512 devices in a mesh: ent: 128 (over x, z, core), rep: 4 (over y).
Axes of the slice: x: 4, y: 4, z: 16, core: 2. Of those that a mesh axis runs over, the one named last changes fastest.
Arguments:
- entity_table: float32 [131072, 200], P('ent'), may hold values from -1.8 to 1.8
- entity_state: float32 [131072], P('ent'), may hold values from 1e-05 to 1
- operators: float32 [256, 200, 200], P('ent'), may hold values from -0.4375 to 0.4375
- operator_state: float32 [256, 200, 200], P('ent'), may hold values from 1 to 100
- sources: int32 [131072], P(('ent', 'rep')), may hold values from 0 to 1023
- destinations: int32 [131072], P(('ent', 'rep')), may hold values from 0 to 1023
- relations: int32 [131072, 1], P(('ent', 'rep')), may hold values from 0 to 255; in each aligned block of 256 rows (0 to 255, 256 to 511, ...) at most 2 rows name the same one
- negatives: int32 [512, 1000], P(('ent', 'rep')), may hold values from 0 to 1023
Outputs:
- new_table: float32 [131072, 200], P('ent')
- new_entity_state: float32 [131072], P('ent')
- new_operators: float32 [256, 200, 200], P('ent')
- new_operator_state: float32 [256, 200, 200], P('ent')
The draws below stay inside these ranges and needn't reach their ends.
Inputs may be any that keep to these rules, and one draw needn't show every extreme that they name: `relations`: among the 256 edges of one device no relation occurs more than 2 times, and some relation occurs exactly 2 times.
All inputs are finite; a program needn't handle non-finite values.
Results may differ from the reference program's by a relative error of at most 0.0019.
Values may be sent and summed in bfloat16 or wider, within the bound.
A program may use at most 64 MiB of HBM per device.

```python
import math
import jax
import jax.numpy as jnp
import numpy as np
from jax import lax

D = 200
NEG = 1000
SPAN = 256
ENT_DEV = 1024
EDGE_DEV = 256
REL = 256
MOST = 2
ENTITIES = 131072
EDGES = 131072
SPANS = 512
N_ENT = 128
N_REP = 4


def place_ends(result, own_key, low, largest):
    place = [jax.random.randint(jax.random.fold_in(own_key, axis), (), 0, length) for axis, length in enumerate(result.shape)]
    widest = result.shape.index(max(result.shape))
    next_to = place[:widest] + [(place[widest] + 1) % result.shape[widest]] + place[widest + 1:]
    return result.at[tuple(place)].set(low).at[tuple(next_to)].set(largest)


def shard_levels(key, shape, shards, least, largest):
    def one(dim, blocks):
        draws = jax.random.uniform(jax.random.fold_in(jax.random.fold_in(key, 6), dim), (blocks,), jnp.float32, least / len(shards), largest / len(shards))
        return jnp.repeat(jnp.exp(draws), shape[dim] // blocks).reshape((-1,) + (1,) * (len(shape) - dim - 1))

    factor_of = one(*shards[0])
    for cut in shards[1:]:
        factor_of = factor_of * one(*cut)
    return factor_of


def deal_out(key, own, number, rows, count, top, limit, slope):
    ranking = jax.random.permutation(key, count)
    crowded, common = shares(count, rows * top, limit, slope, True), shares(count, rows * top, limit, slope, False)
    places = jnp.arange(count)

    def named(tallies, offset_by):
        used = int((tallies > 0).sum())
        fixed = max(1, used // 4)
        shifted = fixed + (places - fixed + offset_by * (used - fixed)) % max(1, count - fixed)
        return jnp.zeros((count,), jnp.int32).at[ranking[jnp.where(places < fixed, places, shifted)]].set(jnp.asarray(tallies, jnp.int32))

    tallies = jnp.where(number % 4 == 0, named(crowded, number // 4), named(common, number - number // 4 - 1))
    mixed = jax.random.permutation(jax.random.fold_in(own, 3), count)
    giver, receiver = mixed[0:count // 2 * 2:2], mixed[1:count // 2 * 2:2]
    margin = jnp.minimum(tallies[giver] - 1, limit - tallies[receiver]) // 2
    margin = jnp.where((giver == ranking[0]) | (receiver == ranking[0]) | (tallies[receiver] == 0), 0, jnp.maximum(margin, 0))
    shifted = jax.random.randint(jax.random.fold_in(own, 4), (count // 2,), 0, 1 << 20) % (margin + 1)
    tallies = tallies.at[giver].add(-shifted).at[receiver].add(shifted)
    members = jnp.searchsorted(jnp.cumsum(tallies), jnp.arange(rows * top), side="right").astype(jnp.int32)
    listing = members.reshape(top, rows).T
    listing = listing[jax.random.permutation(jax.random.fold_in(own, 1), rows)]
    offset_by = jax.random.randint(jax.random.fold_in(own, 2), (rows, 1), 0, top)
    return jnp.take_along_axis(listing, (jnp.arange(top)[None, :] + offset_by) % top, axis=1)


def shares(number_of, total, reach, skew, full):
    loads = [(1 << 20) // math.isqrt(standing ** skew) + 1 for standing in range(1, number_of + 1)]
    largest = reach if full else min(reach, max(-(-total // number_of), total * loads[0] // sum(loads)))
    least = 1 if total - largest >= number_of - 1 else 0
    holding, surplus = [largest] + [least] * (number_of - 1), total - largest - least * (number_of - 1)
    while surplus > 0:
        movable = [i for i in range(1, number_of) if holding[i] < largest] or [i for i in range(1, number_of) if holding[i] < reach]
        mass, budget = sum([loads[i] for i in movable]), surplus
        for i in movable:
            more = min(reach - holding[i], max(1, budget * loads[i] // mass), surplus)
            holding[i] = holding[i] + more
            surplus = surplus - more
    return np.array(holding)


def scatter_about(key, extent, scale, limit, cuts=(), kind=jnp.bfloat16):
    drawn = scale * jax.random.normal(key, extent, jnp.float32)
    if cuts:
        drawn = drawn * shard_levels(key, extent, cuts, -0.22, 0.18)
    return jnp.clip(drawn, -limit, limit).astype(kind)


def setup_inputs(seed: int = 0) -> dict:
    key_of = jax.random.split(jax.random.key(seed), 9)
    entity_table = scatter_about(key_of[0], (ENTITIES, D), 0.3, 1.8, ((0, 128),), jnp.float32)
    entity_state = jnp.clip(jnp.exp(math.log(1.0) - 11.512925 * jax.random.uniform(key_of[1], (ENTITIES,), jnp.float32) ** shard_levels(key_of[1], (ENTITIES,), ((0, 128),), -0.2, 0.2)), 9.999999747378752e-06, 1.0)
    operators = scatter_about(key_of[2], (REL, D, D), D ** -0.5, 0.4375, ((0, 128),), jnp.float32)
    operator_state = jnp.clip(jnp.exp(math.log(100.0) - 4.6051702 * jax.random.uniform(key_of[3], (REL, D, D), jnp.float32) ** shard_levels(key_of[3], (REL, D, D), ((0, 128),), -0.2, 0.2)), 1.0, 100.0)
    sources = place_ends(jax.random.randint(key_of[4], (EDGES,), 0, ENT_DEV), jax.random.fold_in(key_of[4], 1), 0, ENT_DEV - 1).astype(jnp.int32)
    destinations = place_ends(jax.random.randint(key_of[5], (EDGES,), 0, ENT_DEV), jax.random.fold_in(key_of[5], 1), 0, ENT_DEV - 1).astype(jnp.int32)
    relations_keys = jax.random.split(jax.random.fold_in(key_of[6], 1), EDGES // EDGE_DEV)
    relations_turns = jax.random.permutation(jax.random.fold_in(key_of[6], 3), EDGES // EDGE_DEV)
    relations = jax.vmap(lambda own, number: deal_out(jax.random.fold_in(key_of[6], 2), own, number, EDGE_DEV, REL, 1, MOST, 2))(relations_keys, relations_turns).reshape((EDGES, 1))
    negatives = place_ends(jax.random.randint(key_of[7], (SPANS, NEG), 0, ENT_DEV), jax.random.fold_in(key_of[7], 1), 0, ENT_DEV - 1).astype(jnp.int32)
    return {"entity_table": entity_table, "entity_state": entity_state, "operators": operators, "operator_state": operator_state, "sources": sources, "destinations": destinations, "relations": relations, "negatives": negatives}


entity_rate = 0.1
operator_rate = 0.02
epsilon = 1e-06

def place_slots(relation_ids, capacity):
    count_edges = relation_ids.shape[0]
    ordering = jnp.argsort(relation_ids, stable=True).astype(jnp.int32)
    ranked = relation_ids[ordering]
    leading = jnp.searchsorted(ranked, ranked, side='left').astype(jnp.int32)
    within = jnp.arange(count_edges, dtype=jnp.int32) - leading
    position = jnp.zeros((count_edges,), jnp.int32).at[ordering].set(within)
    return relation_ids * capacity + position

def score_grads(transformed, target_ids, negative_ids, table_rows):
    target_rows = jnp.take(table_rows, target_ids, axis=0)
    positive = lax.optimization_barrier(jnp.sum(transformed.astype(jnp.float32) * target_rows.astype(jnp.float32), axis=-1))
    positive_grad = -jax.nn.sigmoid(-positive)
    width = transformed.shape[1]
    blocks = transformed.reshape(-1, SPAN, width)
    negative_count = negative_ids.shape[1]

    def span_step(running, pieces):
        query_block, negative_block = pieces
        negative_rows = jnp.take(table_rows, negative_block, axis=0)
        scores = lax.dot_general(query_block, negative_rows, (((1,), (1,)), ((), ())), preferred_element_type=jnp.float32)
        negative_grad = (jax.nn.sigmoid(scores) / negative_count).astype(jnp.bfloat16)
        query_part = jnp.dot(negative_grad, negative_rows, preferred_element_type=jnp.float32)
        row_update = lax.dot_general(negative_grad, query_block, (((0,), (0,)), ((), ())), preferred_element_type=jnp.float32)
        return (running.at[negative_block].add(row_update), query_part)
    starting = jnp.zeros((table_rows.shape[0], width), jnp.float32)
    negative_total, query_parts = lax.scan(span_step, starting, (blocks, negative_ids))
    query_grad = (positive_grad[:, None] * target_rows.astype(jnp.float32) + query_parts.reshape(-1, width)).astype(jnp.bfloat16)
    target_grad = negative_total.at[target_ids].add(positive_grad[:, None] * transformed.astype(jnp.float32))
    return (query_grad, target_grad)

def row_adagrad(weights, moments, gradient):
    fresh_moments = moments + lax.optimization_barrier(jnp.mean(gradient * gradient, axis=-1))
    updated = weights - entity_rate * gradient / (jnp.sqrt(fresh_moments)[:, None] + epsilon)
    return (updated, fresh_moments)

def dense_adagrad(weights, moments, gradient):
    fresh_moments = moments + gradient * gradient
    updated = weights - operator_rate * gradient / (jnp.sqrt(fresh_moments) + epsilon)
    return (updated, fresh_moments)

def reference(entity_table, entity_state, operators, operator_state, sources, destinations, relations, negatives):
    table_half = entity_table.astype(jnp.bfloat16)
    operators_wide = operators.astype(jnp.bfloat16).astype(jnp.float32)
    span_rows = EDGE_DEV // SPAN

    def block_step(running, block):
        entity_grad, operator_grad = running
        partition = block // N_REP
        following = (partition + 1) % N_ENT
        source_table = lax.dynamic_slice_in_dim(table_half, partition * ENT_DEV, ENT_DEV, 0)
        target_table = lax.dynamic_slice_in_dim(table_half, following * ENT_DEV, ENT_DEV, 0)
        source_ids = lax.dynamic_slice_in_dim(sources, block * EDGE_DEV, EDGE_DEV, 0)
        target_ids = lax.dynamic_slice_in_dim(destinations, block * EDGE_DEV, EDGE_DEV, 0)
        relation_ids = lax.dynamic_slice_in_dim(relations[:, 0], block * EDGE_DEV, EDGE_DEV, 0)
        negative_ids = lax.dynamic_slice_in_dim(negatives, block * span_rows, span_rows, 0)
        slot_index = place_slots(relation_ids, MOST)
        source_rows = jnp.take(source_table, source_ids, axis=0)
        outgoing = jnp.zeros((REL * MOST, D), jnp.bfloat16).at[slot_index].set(source_rows).reshape(REL, MOST, D)
        transformed_slots = jnp.einsum('rmd,rdk->rmk', outgoing.astype(jnp.float32), operators_wide).astype(jnp.bfloat16)
        transformed = jnp.take(transformed_slots.reshape(REL * MOST, D), slot_index, axis=0)
        query_grad, target_grad = score_grads(transformed, target_ids, negative_ids, target_table)
        grad_slots = jnp.zeros((REL * MOST, D), jnp.bfloat16).at[slot_index].set(query_grad).reshape(REL, MOST, D)
        source_slots = jnp.einsum('rmk,rdk->rmd', grad_slots.astype(jnp.float32), operators_wide).astype(jnp.bfloat16)
        source_grad = jnp.take(source_slots.reshape(REL * MOST, D), slot_index, axis=0)
        operator_grad = operator_grad + jnp.einsum('rmd,rmk->rdk', outgoing.astype(jnp.float32), grad_slots.astype(jnp.float32))
        entity_grad = entity_grad.at[partition * ENT_DEV + source_ids].add(source_grad.astype(jnp.float32))
        current = lax.dynamic_slice_in_dim(entity_grad, following * ENT_DEV, ENT_DEV, 0)
        entity_grad = lax.dynamic_update_slice_in_dim(entity_grad, current + target_grad, following * ENT_DEV, 0)
        return ((entity_grad, operator_grad), None)
    starting = (jnp.zeros((ENTITIES, D), jnp.float32), jnp.zeros((REL, D, D), jnp.float32))
    (entity_grad, operator_grad), _ = lax.scan(block_step, starting, jnp.arange(N_ENT * N_REP, dtype=jnp.int32))
    new_table, new_entity_state = row_adagrad(entity_table, entity_state, entity_grad)
    new_operators, new_operator_state = dense_adagrad(operators, operator_state, operator_grad)
    return (new_table, new_entity_state, new_operators, new_operator_state)
```

```python
import functools

import jax
import jax.numpy as jnp
from jax import lax
from jax.experimental import pallas as pl
from jax.experimental.pallas import tpu as pltpu
from jax.sharding import PartitionSpec as P

MESH = pl.DeviceIdType.MESH
F32 = jnp.float32
BF16 = jnp.bfloat16

D = 200
NEG = 1000
ROWS = 1024
EDGES = 256
PEERS = 128
REPS = 4
DEPTH = 16
HALF = 112

entity_rate = 0.1
operator_rate = 0.02
epsilon = 1e-06


def dot(a, b):
    return jnp.dot(a, b, preferred_element_type=F32)


def dot_nt(a, b):
    return lax.dot_general(a, b, (((1,), (1,)), ((), ())), preferred_element_type=F32)


def one_hot(index, iota):
    return jnp.where(iota == index, 1.0, 0.0).astype(BF16)


def column(row):
    return jnp.transpose(jnp.broadcast_to(row, (128, row.shape[1])))[:, :1]


def places(relation):
    row = jnp.broadcast_to(relation, (EDGES, EDGES))
    col = jnp.transpose(row)
    sub = lax.broadcasted_iota(jnp.int32, (EDGES, EDGES), 0)
    lane = lax.broadcasted_iota(jnp.int32, (EDGES, EDGES), 1)
    same = jnp.where(row == col, 1.0, 0.0)
    before_row = jnp.sum(jnp.where(sub < lane, same, 0.0), axis=0, keepdims=True)
    before_col = jnp.sum(jnp.where(lane < sub, same, 0.0), axis=1, keepdims=True)

    def spot(rel, before):
        slot = rel * 2 + before.astype(jnp.int32)
        return (slot // 4) * 8 + lax.rem(slot, 4)

    return spot(relation, before_row), spot(col[:, :1], before_col)


def spread(place_row):
    iota = lax.broadcasted_iota(jnp.int32, (8 * PEERS, EDGES), 0)
    return one_hot(place_row, iota), one_hot(place_row + 4, iota)


def collect(place_col):
    iota = lax.broadcasted_iota(jnp.int32, (EDGES, 8 * PEERS), 1)
    return one_hot(place_col, iota), one_hot(place_col + 4, iota)


def partner(me, i):
    step = (PEERS - i) // 8
    rest = lax.rem(PEERS - i, 8)
    odd = lax.rem(step, 2)
    hop = odd * ((step + 1) // 2) + (1 - odd) * (DEPTH - step // 2)
    x, z, c = me // (2 * DEPTH), lax.rem(me // 2, DEPTH), lax.rem(me, 2)
    return (lax.rem(x + rest // 2, 4) * DEPTH + lax.rem(z + hop, DEPTH)) * 2 + lax.rem(c + rest, 2)


def exchange(me, source, target, own, from_at, to_at, sends, arrivals):
    def send(i, _):
        peer = partner(me, i)
        pltpu.make_async_remote_copy(
            source.at[from_at(peer)],
            target.at[to_at],
            sends,
            arrivals,
            device_id={"ent": peer},
            device_id_type=MESH,
        ).start()
        return 0

    lax.fori_loop(1, PEERS, send, 0)
    target[own] = source[from_at(me)]


def all_of(ref, count, sends, arrivals, axis, me):
    part = ref.at[pl.ds(0, count)]
    return pltpu.make_async_remote_copy(
        part, part, sends, arrivals, device_id={axis: me}, device_id_type=MESH
    )


def kernel(
    table_ref, state_ref, ops_ref, opstate_ref, src_ref, dst_ref, rel_ref, neg_ref,
    table_out, state_out, ops_out, opstate_out,
    half, ops_half, negs, there_dst, there_rel, there_neg, there_src,
    send1, recv1, send2, recv2, send3, recv3, send4, recv4,
    rows_first, hits, tg_send, tg_recv, tg_all, og_send, og_recv, og_all, sg_all,
    ssem, rsem,
):
    me = lax.axis_index("ent")
    y = lax.axis_index("rep")
    nxt = lax.rem(me + 1, PEERS)
    prev = lax.rem(me + PEERS - 1, PEERS)

    barrier = pltpu.get_barrier_semaphore()

    def greet(i, _):
        pl.semaphore_signal(
            barrier, inc=1, device_id={"ent": lax.rem(me + i, PEERS)}, device_id_type=MESH
        )
        return 0

    lax.fori_loop(1, PEERS, greet, 0)
    for i in range(1, REPS):
        pl.semaphore_signal(
            barrier, inc=1, device_id={"rep": lax.rem(y + i, REPS)}, device_id_type=MESH
        )

    def to_reps(source_at, target_at, sem):
        for i in range(1, REPS):
            other = lax.rem(y + i, REPS)
            pltpu.make_async_remote_copy(
                source_at(other), target_at, ssem.at[sem], rsem.at[sem],
                device_id={"rep": other}, device_id_type=MESH,
            ).start()

    half[...] = jnp.zeros_like(half)
    half[0:D, :] = table_ref[...].astype(BF16)
    ops_half[...] = jnp.zeros_like(ops_half)
    for r in range(2):
        ops_half[r, 0:D, 0:D] = ops_ref[r].astype(BF16)
    negs[...] = jnp.full_like(negs, -1)
    negs[:, 0:NEG] = neg_ref[...]
    there_src[y] = src_ref[...]

    place_row, place_col = places(rel_ref[...])
    low, high = spread(place_row)
    picked = one_hot(src_ref[...], lax.broadcasted_iota(jnp.int32, (ROWS, EDGES), 0))
    source_rows = dot(half[...], picked).astype(BF16)
    send1[...] = (
        (dot_nt(low, source_rows[0:128]) + dot_nt(high, source_rows[128:256]))
        .reshape(PEERS, 8, 128)
        .astype(BF16)
    )

    pl.semaphore_wait(barrier, PEERS - 1 + REPS - 1)

    shifted = [
        pltpu.make_async_remote_copy(
            a, b, ssem.at[k], rsem.at[k], device_id={"ent": nxt}, device_id_type=MESH
        )
        for a, b, k in ((dst_ref, there_dst, 4), (rel_ref, there_rel, 5), (negs, there_neg, 6))
    ]
    for copy in shifted:
        copy.start()
    exchange(me, send1, recv1, me, lambda p: p, me, ssem.at[0], rsem.at[0])
    to_reps(lambda other: src_ref, there_src.at[y], 7)

    def regroup(h):
        i = lax.broadcasted_iota(jnp.int32, (512, 1024), 0)
        place = (lax.rem(i, 256) // 2) * 8 + h * 4 + (i // 256) * 2 + lax.rem(i, 2)
        return one_hot(place, lax.broadcasted_iota(jnp.int32, (512, 1024), 1))

    def ungroup(h):
        i = lax.broadcasted_iota(jnp.int32, (1024, 512), 1)
        place = (lax.rem(i, 256) // 2) * 8 + h * 4 + (i // 256) * 2 + lax.rem(i, 2)
        return one_hot(place, lax.broadcasted_iota(jnp.int32, (1024, 512), 0))

    group = [regroup(0), regroup(1)]
    back = [ungroup(0), ungroup(1)]

    def grouped(ref):
        flat = ref[...].astype(F32).reshape(8 * PEERS, 128).astype(BF16)
        return jnp.concatenate([dot(group[0], flat), dot(group[1], flat)], axis=1)

    def ungrouped(value):
        value = value.astype(BF16)
        return (
            (dot(back[0], value[:, 0:128]) + dot(back[1], value[:, 128:256]))
            .reshape(PEERS, 8, 128)
            .astype(BF16)
        )

    all_of(recv1, PEERS - 1, ssem.at[0], rsem.at[0], "ent", me).wait_recv()
    rows1 = grouped(recv1)
    rows1_half = rows1.astype(BF16)
    send2[...] = ungrouped(
        jnp.concatenate(
            [dot(rows1_half[256 * r : 256 * r + 256], ops_half[r]) for r in range(2)], axis=0
        )
    )
    exchange(
        me, send2, recv2, me, lambda p: lax.rem(p + PEERS - 1, PEERS), me, ssem.at[1], rsem.at[1]
    )
    for r in range(2):
        rows_first[r] = jnp.transpose(rows1[256 * r : 256 * r + 256]).astype(BF16)

    for copy in shifted:
        copy.wait_recv()
    all_of(there_src, REPS - 1, ssem.at[7], rsem.at[7], "rep", y).wait_recv()
    far_row, far_col = places(there_rel[...])
    far_low, far_high = spread(far_row)
    take_low, take_high = collect(far_col)
    wide = lax.broadcasted_iota(jnp.int32, (EDGES, ROWS), 1)
    is_target = column(there_dst[...]) == wide
    for k in range(REPS):
        hits[k] = one_hot(column(there_src[k]), wide)
    named = there_neg[...]
    coarse = one_hot(named >> 7, lax.broadcasted_iota(jnp.int32, (8, ROWS), 0))
    fine = one_hot(named & 127, lax.broadcasted_iota(jnp.int32, (128, ROWS), 0))
    tally = dot_nt(coarse, fine)
    tally = jnp.concatenate([tally[j : j + 1] for j in range(8)], axis=1)

    all_of(recv2, PEERS - 1, ssem.at[1], rsem.at[1], "ent", me).wait_recv()
    flat2 = recv2[...].astype(F32).reshape(8 * PEERS, 128).astype(BF16)
    moved = jnp.concatenate([dot(take_low, flat2), dot(take_high, flat2)], axis=1)
    moved_half = moved.astype(BF16)
    scores = dot(moved_half, half[...])
    positive = jnp.sum(jnp.where(is_target, scores, 0.0), axis=1, keepdims=True)
    positive_grad = -jax.nn.sigmoid(-positive)
    weight = (tally * (jax.nn.sigmoid(scores) * (1.0 / NEG))).astype(BF16)
    target_hot = jnp.where(is_target, 1.0, 0.0).astype(BF16)
    query_grad = positive_grad * dot_nt(target_hot, half[...]) + dot_nt(weight, half[...])
    query_half = query_grad.astype(BF16)
    send3[...] = (
        (dot(far_low, query_half[:, 0:128]) + dot(far_high, query_half[:, 128:256]))
        .reshape(PEERS, 8, 128)
        .astype(BF16)
    )
    exchange(me, send3, recv3, prev, lambda p: p, prev, ssem.at[2], rsem.at[2])

    target_grad = dot(jnp.transpose(moved).astype(BF16), weight) + dot(
        jnp.transpose(positive_grad * moved).astype(BF16), target_hot
    )
    for k in range(REPS):
        tg_send[k] = target_grad[0:D, 256 * k : 256 * k + 256].astype(BF16)
    to_reps(lambda other: tg_send.at[other], tg_recv.at[y], 8)
    take_low, take_high = collect(place_col)
    all_of(tg_recv, REPS - 1, ssem.at[8], rsem.at[8], "rep", y).wait_recv()
    total = tg_send[y].astype(F32)
    for i in range(1, REPS):
        total = total + tg_recv[lax.rem(y + i, REPS)].astype(F32)
    tg_all[y] = total.astype(BF16)
    to_reps(lambda other: tg_all.at[y], tg_all.at[y], 9)

    all_of(recv3, PEERS - 1, ssem.at[2], rsem.at[2], "ent", me).wait_recv()
    rows3 = grouped(recv3).astype(BF16)
    send4[...] = ungrouped(
        jnp.concatenate(
            [dot_nt(rows3[256 * r : 256 * r + 256], ops_half[r]) for r in range(2)], axis=0
        )
    )
    exchange(me, send4, recv4, me, lambda p: p, me, ssem.at[3], rsem.at[3])
    for r in range(2):
        operator_grad = dot(rows_first[r], rows3[256 * r : 256 * r + 256])
        og_send[2 * r] = operator_grad[0:HALF].astype(BF16)
        og_send[2 * r + 1] = operator_grad[HALF : 2 * HALF].astype(BF16)
    to_reps(lambda other: og_send.at[other], og_recv.at[y], 10)
    all_of(og_recv, REPS - 1, ssem.at[10], rsem.at[10], "rep", y).wait_recv()
    total = og_send[y].astype(F32)
    for i in range(1, REPS):
        total = total + og_recv[lax.rem(y + i, REPS)].astype(F32)
    og_all[y] = total.astype(BF16)
    to_reps(lambda other: og_all.at[y], og_all.at[y], 11)
    all_of(og_all, REPS - 1, ssem.at[11], rsem.at[11], "rep", y).wait_recv()
    for r in range(2):
        for part, (low_row, high_row) in enumerate(((0, HALF), (HALF, D))):
            gradient = og_all[2 * r + part][0 : high_row - low_row, 0:D].astype(F32)
            fresh = opstate_ref[r, low_row:high_row, :] + gradient * gradient
            opstate_out[r, low_row:high_row, :] = fresh
            ops_out[r, low_row:high_row, :] = ops_ref[r, low_row:high_row, :] - (
                operator_rate * gradient / (jnp.sqrt(fresh) + epsilon)
            )
    all_of(tg_all, REPS - 1, ssem.at[9], rsem.at[9], "rep", y).wait_recv()

    all_of(recv4, PEERS - 1, ssem.at[3], rsem.at[3], "ent", me).wait_recv()
    flat4 = recv4[...].astype(F32).reshape(8 * PEERS, 128).astype(BF16)
    source_grad = jnp.concatenate([dot(take_low, flat4), dot(take_high, flat4)], axis=1)
    sg_all[y] = jnp.transpose(source_grad)[0:D].astype(BF16)
    to_reps(lambda other: sg_all.at[y], sg_all.at[y], 12)
    all_of(sg_all, REPS - 1, ssem.at[12], rsem.at[12], "rep", y).wait_recv()
    gradient = jnp.concatenate([tg_all[k].astype(F32) for k in range(REPS)], axis=1)
    for k in range(REPS):
        gradient = gradient + dot(sg_all[k], hits[k])
    fresh = state_ref[...] + jnp.sum(gradient * gradient, axis=0, keepdims=True) * (1.0 / D)
    state_out[...] = fresh
    table_out[...] = table_ref[...] - gradient * (entity_rate / (jnp.sqrt(fresh) + epsilon))

    for k, buffer in enumerate((send1, send2, send3, send4)):
        all_of(buffer, PEERS - 1, ssem.at[k], rsem.at[k], "ent", me).wait_send()
    for copy in shifted:
        copy.wait_send()
    for k, buffer in (
        (7, there_src), (8, tg_send), (9, tg_all), (10, og_send), (11, og_all), (12, sg_all)
    ):
        all_of(buffer, REPS - 1, ssem.at[k], rsem.at[k], "rep", y).wait_send()


def shards(
    entity_table,
    entity_state,
    operators,
    operator_state,
    sources,
    destinations,
    relations,
    negatives,
):
    vmem = pl.BlockSpec(memory_space=pltpu.VMEM)
    blocks = pltpu.VMEM((PEERS, 8, 128), BF16)
    table, state, ops, opstate = pl.pallas_call(
        kernel,
        name="step",
        out_shape=(
            jax.ShapeDtypeStruct((D, ROWS), F32),
            jax.ShapeDtypeStruct((1, ROWS), F32),
            jax.ShapeDtypeStruct((2, D, D), F32),
            jax.ShapeDtypeStruct((2, D, D), F32),
        ),
        in_specs=[vmem] * 8,
        out_specs=(vmem,) * 4,
        scratch_shapes=[
            pltpu.VMEM((256, ROWS), BF16),
            pltpu.VMEM((2, 256, 256), BF16),
            pltpu.VMEM((1, ROWS), jnp.int32),
            pltpu.VMEM((1, EDGES), jnp.int32),
            pltpu.VMEM((1, EDGES), jnp.int32),
            pltpu.VMEM((1, ROWS), jnp.int32),
            pltpu.VMEM((REPS, 1, EDGES), jnp.int32),
            *([blocks] * 8),
            pltpu.VMEM((2, 256, 256), BF16),
            pltpu.VMEM((REPS, EDGES, ROWS), BF16),
            *([pltpu.VMEM((REPS, D, 256), BF16)] * 3),
            *([pltpu.VMEM((REPS, HALF, 256), BF16)] * 3),
            pltpu.VMEM((REPS, D, 256), BF16),
            pltpu.SemaphoreType.DMA((13,)),
            pltpu.SemaphoreType.DMA((13,)),
        ],
        compiler_params=pltpu.CompilerParams(
            collective_id=0, has_side_effects=True, vmem_limit_bytes=48 << 20
        ),
    )(
        entity_table.T,
        entity_state.reshape(1, ROWS),
        operators,
        operator_state,
        sources.reshape(1, EDGES),
        destinations.reshape(1, EDGES),
        relations.reshape(1, EDGES),
        negatives,
    )
    return (table.T, state.reshape(ROWS), ops, opstate)


def solution(mesh):
    placed = (
        P("ent", None),
        P("ent"),
        P("ent", None, None),
        P("ent", None, None),
        P(("ent", "rep")),
        P(("ent", "rep")),
        P(("ent", "rep"), None),
        P(("ent", "rep"), None),
    )
    return jax.shard_map(
        shards,
        mesh=mesh,
        in_specs=placed,
        out_specs=(P("ent", None), P("ent"), P("ent", None, None), P("ent", None, None)),
        check_vma=False,
    )
```

```python
import jax
import jax.numpy as jnp
from jax import lax
from jax.experimental import pallas as pl
from jax.experimental.pallas import tpu as pltpu
from jax.sharding import PartitionSpec as P

MESH = pl.DeviceIdType.MESH
F32 = jnp.float32
BF16 = jnp.bfloat16

D = 200
NEG = 1000
ROWS = 1024
EDGES = 256
PEERS = 128
REPS = 4
DEPTH = 16
HALF = 112
CHUNKS = 4
BLOCKS = PEERS // CHUNKS
SLOTS = 4 * BLOCKS

entity_rate = 0.1
operator_rate = 0.02
epsilon = 1e-06


def dot(a, b):
    return jnp.dot(a, b, preferred_element_type=F32)


def dot_nt(a, b):
    return lax.dot_general(a, b, (((1,), (1,)), ((), ())), preferred_element_type=F32)


def one_hot(index, shape, axis):
    return jnp.where(lax.broadcasted_iota(jnp.int32, shape, axis) == index, 1.0, 0.0).astype(BF16)


def column(row):
    return jnp.transpose(jnp.broadcast_to(row, (128, row.shape[1])))[:, :1]


def split(device):
    return device // (2 * DEPTH), lax.rem(device // 2, DEPTH), lax.rem(device, 2)


def offset(k):
    step, rest = k // 8, lax.rem(k, 8)
    odd = lax.rem(step, 2)
    hop = odd * (7 - step // 2) + (1 - odd) * (8 + step // 2)
    return rest // 2, hop, lax.rem(rest, 2)


def ahead(device, k):
    x, z, c = split(device)
    dx, dz, dc = offset(k)
    return (lax.rem(x + dx, 4) * DEPTH + lax.rem(z + dz, DEPTH)) * 2 + lax.rem(c + dc, 2)


def behind(device, k):
    x, z, c = split(device)
    dx, dz, dc = offset(k)
    return (lax.rem(x + 4 - dx, 4) * DEPTH + lax.rem(z + DEPTH - dz, DEPTH)) * 2 + lax.rem(
        c + dc, 2
    )


def slot_of(relation, device):
    row = jnp.broadcast_to(relation, (EDGES, EDGES))
    col = jnp.transpose(row)
    sub = lax.broadcasted_iota(jnp.int32, (EDGES, EDGES), 0)
    lane = lax.broadcasted_iota(jnp.int32, (EDGES, EDGES), 1)
    earlier = jnp.sum(
        jnp.where((row == col) & (sub < lane), 1.0, 0.0), axis=0, keepdims=True
    ).astype(jnp.int32)
    x, z, c = split(device)
    owner = relation >> 1
    dx = ((owner >> 5) + 4 - x) & 3
    dz = (((owner >> 1) & 15) + DEPTH - z) & 15
    dc = ((owner & 1) + 2 - c) & 1
    step = jnp.where(dz >= 8, 2 * (dz - 8), 15 - 2 * dz)
    k = step * 8 + dx * 2 + dc
    return (k >> 5) * SLOTS + (relation & 1) * (2 * BLOCKS) + (k & 31) * 2 + earlier


def block_row(i):
    slot = i & 127
    return ((slot & 63) >> 1) * 8 + (i >> 7) * 4 + (slot >> 6) * 2 + (slot & 1)


def step_kernel(
    table_hbm, state_hbm, ops_hbm, opstate_hbm, src_hbm, dst_hbm, rel_hbm, neg_hbm,
    table_out, state_out, ops_out, opstate_out,
    table, state, ops, opstate, src, dst, rel, neg,
    half, ops_half, negs, there_dst, there_rel, there_neg, there_src,
    send1, recv1, send2, recv2, send3, recv3, send4, recv4,
    rows_first, rows_third, moved_all, pulled_all, weights, target_hot, target_rows,
    hits, tg_send, tg_recv, tg_all, og_send, og_recv, og_all, sg_all,
    lsem, ssem, rsem, xsend, xrecv,
):
    me = lax.axis_index("ent")
    y = lax.axis_index("rep")
    nxt = lax.rem(me + 1, PEERS)
    prev = lax.rem(me + PEERS - 1, PEERS)

    loads = [
        pltpu.make_async_copy(a, b, lsem.at[i])
        for i, (a, b) in enumerate(
            (
                (rel_hbm, rel), (src_hbm, src), (dst_hbm, dst),
                (neg_hbm, neg), (table_hbm, table), (ops_hbm, ops),
                (opstate_hbm, opstate), (state_hbm, state),
            )
        )
    ]
    for load in loads:
        load.start()

    barrier = pltpu.get_barrier_semaphore()

    def greet(i, _):
        pl.semaphore_signal(
            barrier, inc=1, device_id={"ent": lax.rem(me + i, PEERS)}, device_id_type=MESH
        )
        return 0

    lax.fori_loop(1, PEERS, greet, 0)
    for i in range(1, REPS):
        pl.semaphore_signal(
            barrier, inc=1, device_id={"rep": lax.rem(y + i, REPS)}, device_id_type=MESH
        )

    def to_reps(source_at, target_at, sem):
        for i in range(1, REPS):
            other = lax.rem(y + i, REPS)
            pltpu.make_async_remote_copy(
                source_at(other), target_at, ssem.at[sem], rsem.at[sem],
                device_id={"rep": other}, device_id_type=MESH,
            ).start()

    def from_reps(ref, sem):
        part = ref.at[pl.ds(0, REPS - 1)]
        return pltpu.make_async_remote_copy(
            part, part, ssem.at[sem], rsem.at[sem], device_id={"rep": y}, device_id_type=MESH
        )

    def send_chunk(phase, g, source, target, peer_of):
        def send(i, _):
            k = g * BLOCKS + i
            peer = peer_of(k)

            @pl.when(peer != me)
            def _():
                pltpu.make_async_remote_copy(
                    source.at[k], target.at[k],
                    xsend.at[phase], xrecv.at[phase * CHUNKS + g],
                    device_id={"ent": peer}, device_id_type=MESH,
                ).start()

            @pl.when(peer == me)
            def _():
                pltpu.make_async_copy(
                    source.at[k], target.at[k], xrecv.at[phase * CHUNKS + g]
                ).start()

            return 0

        lax.fori_loop(0, BLOCKS, send, 0)

    def wait_chunk(phase, g, target):
        part = target.at[pl.ds(g * BLOCKS, BLOCKS)]
        pltpu.make_async_copy(part, part, xrecv.at[phase * CHUNKS + g]).wait()

    for load in loads[:4]:
        load.wait()
    negs[...] = jnp.full_like(negs, -1)
    negs[:, 0:NEG] = neg[...]
    there_src[y] = src[...]
    slots = slot_of(rel[...], me)
    pack = one_hot(
        block_row(lax.broadcasted_iota(jnp.int32, (8 * BLOCKS, 2 * SLOTS), 1)),
        (8 * BLOCKS, 2 * SLOTS), 0,
    )
    unpack = one_hot(
        block_row(lax.broadcasted_iota(jnp.int32, (2 * SLOTS, 8 * BLOCKS), 0)),
        (2 * SLOTS, 8 * BLOCKS), 1,
    )

    def put(ref, g, value):
        value = value.astype(BF16)
        stacked = jnp.concatenate([value[:, 0:128], value[:, 128:256]], axis=0)
        ref[g * BLOCKS : (g + 1) * BLOCKS] = (
            dot(pack, stacked).reshape(BLOCKS, 8, 128).astype(BF16)
        )

    def get(ref, g):
        flat = ref[g * BLOCKS : (g + 1) * BLOCKS].astype(F32).reshape(8 * BLOCKS, 128)
        both = dot(unpack, flat.astype(BF16))
        return jnp.concatenate([both[0:SLOTS], both[SLOTS : 2 * SLOTS]], axis=1)

    picked = one_hot(src[...], (ROWS, EDGES), 0)
    half[...] = jnp.zeros_like(half)
    ops_half[...] = jnp.zeros_like(ops_half)
    loads[4].wait()
    half[0:D, :] = table[...].astype(BF16)
    source_rows = dot(half[...], picked).astype(BF16)
    for g in range(CHUNKS):
        here = one_hot(slots - g * SLOTS, (SLOTS, EDGES), 0)
        put(send1, g, dot_nt(here, source_rows))

    pl.semaphore_wait(barrier, PEERS - 1 + REPS - 1)

    for g in range(CHUNKS):
        send_chunk(0, g, send1, recv1, lambda k: ahead(me, k))
    shifted = [
        pltpu.make_async_remote_copy(
            a, b, ssem.at[i], rsem.at[i], device_id={"ent": nxt}, device_id_type=MESH
        )
        for i, (a, b) in enumerate(((dst, there_dst), (rel, there_rel), (negs, there_neg)))
    ]
    for copy in shifted:
        copy.start()
    to_reps(lambda other: src, there_src.at[y], 3)

    loads[5].wait()
    for r in range(2):
        ops_half[r, 0:D, 0:D] = ops[r].astype(BF16)
    for copy in shifted:
        copy.wait_recv()
    far_slots = slot_of(there_rel[...], prev)
    for g in range(CHUNKS):
        here = (
            lax.broadcasted_iota(jnp.int32, (SLOTS, EDGES), 0) == far_slots - g * SLOTS
        )
        target = (
            jnp.sum(
                jnp.where(here, (there_dst[...] + 1).astype(F32), 0.0), axis=1, keepdims=True
            ).astype(jnp.int32)
            - 1
        )
        hot = one_hot(target, (SLOTS, ROWS), 1)
        target_hot[g * SLOTS : (g + 1) * SLOTS] = hot
    target_rows[...] = dot_nt(target_hot[...], half[...])
    named = there_neg[...]
    coarse = one_hot(named >> 7, (8, ROWS), 0)
    fine = one_hot(named & 127, (128, ROWS), 0)
    tally = dot_nt(coarse, fine) * (1.0 / NEG)
    tally = jnp.concatenate([tally[j : j + 1] for j in range(8)], axis=1)

    for g in range(CHUNKS):
        wait_chunk(0, g, recv1)
        rows = get(recv1, g).astype(BF16)
        put(
            send2, g,
            jnp.concatenate(
                [dot(rows[64 * r : 64 * r + 64], ops_half[r]) for r in range(2)], axis=0
            ),
        )
        send_chunk(1, g, send2, recv2, lambda k: lax.rem(behind(me, k) + 1, PEERS))
        for r in range(2):
            rows_first[r, 64 * g : 64 * g + 64] = rows[64 * r : 64 * r + 64]

    from_reps(there_src, 3).wait_recv()
    for k in range(REPS):
        hits[k] = one_hot(column(there_src[k]), (EDGES, ROWS), 1)

    for g in range(CHUNKS):
        span = slice(g * SLOTS, (g + 1) * SLOTS)
        wait_chunk(1, g, recv2)
        moved = get(recv2, g)
        moved_half = moved.astype(BF16)
        scores = dot(moved_half, half[...])
        positive = jnp.sum(
            jnp.where(target_hot[span] > 0, scores, 0.0), axis=1, keepdims=True
        )
        positive_grad = -jax.nn.sigmoid(-positive)
        weight = (tally * jax.nn.sigmoid(scores)).astype(BF16)
        put(send3, g, positive_grad * target_rows[span] + dot_nt(weight, half[...]))
        send_chunk(2, g, send3, recv3, lambda k: ahead(prev, k))
        weights[span] = weight
        moved_all[span] = moved_half
        pulled_all[span] = (positive_grad * moved).astype(BF16)

    def turned(ref):
        return jnp.transpose(ref.astype(F32)).astype(BF16)

    target_grad = dot(turned(moved_all[...]), weights[...]) + dot(
        turned(pulled_all[...]), target_hot[...]
    )
    for k in range(REPS):
        tg_send[k] = target_grad[0:D, 256 * k : 256 * k + 256].astype(BF16)
    to_reps(lambda other: tg_send.at[other], tg_recv.at[y], 4)

    for g in range(CHUNKS):
        wait_chunk(2, g, recv3)
        rows = get(recv3, g).astype(BF16)
        put(
            send4, g,
            jnp.concatenate(
                [dot_nt(rows[64 * r : 64 * r + 64], ops_half[r]) for r in range(2)], axis=0
            ),
        )
        send_chunk(3, g, send4, recv4, lambda k: behind(me, k))
        for r in range(2):
            rows_third[r, 64 * g : 64 * g + 64] = rows[64 * r : 64 * r + 64]

    def summed(sent, received):
        total = sent[y].astype(F32)
        for i in range(1, REPS):
            total = total + received[lax.rem(y + i, REPS)].astype(F32)
        return total.astype(BF16)

    from_reps(tg_recv, 4).wait_recv()
    tg_all[y] = summed(tg_send, tg_recv)
    to_reps(lambda other: tg_all.at[y], tg_all.at[y], 5)
    for r in range(2):
        operator_grad = dot(turned(rows_first[r]), rows_third[r])
        og_send[2 * r] = operator_grad[0:HALF].astype(BF16)
        og_send[2 * r + 1] = operator_grad[HALF : 2 * HALF].astype(BF16)
    to_reps(lambda other: og_send.at[other], og_recv.at[y], 6)
    slot_col = column(slots)
    takes = [one_hot(slot_col - g * SLOTS, (EDGES, SLOTS), 1) for g in range(CHUNKS)]
    from_reps(og_recv, 6).wait_recv()
    og_all[y] = summed(og_send, og_recv)
    to_reps(lambda other: og_all.at[y], og_all.at[y], 7)

    loads[6].wait()
    loads[7].wait()
    from_reps(og_all, 7).wait_recv()
    for r in range(2):
        for part, (low, high) in enumerate(((0, HALF), (HALF, D))):
            gradient = og_all[2 * r + part][0 : high - low, 0:D].astype(F32)
            fresh = opstate[r, low:high, :] + gradient * gradient
            opstate_out[r, low:high, :] = fresh
            ops_out[r, low:high, :] = ops[r, low:high, :] - (
                operator_rate * gradient / (jnp.sqrt(fresh) + epsilon)
            )
    from_reps(tg_all, 5).wait_recv()

    source_grad = jnp.zeros((EDGES, 256), F32)
    for g in range(CHUNKS):
        wait_chunk(3, g, recv4)
        source_grad = source_grad + dot(takes[g], get(recv4, g).astype(BF16))
    sg_all[y] = jnp.transpose(source_grad)[0:D].astype(BF16)
    to_reps(lambda other: sg_all.at[y], sg_all.at[y], 8)

    gradient = jnp.concatenate([tg_all[k].astype(F32) for k in range(REPS)], axis=1)
    from_reps(sg_all, 8).wait_recv()
    for k in range(REPS):
        gradient = gradient + dot(sg_all[k], hits[k])
    fresh = state[...] + jnp.sum(gradient * gradient, axis=0, keepdims=True) * (1.0 / D)
    state_out[...] = fresh
    table_out[...] = table[...] - gradient * (entity_rate / (jnp.sqrt(fresh) + epsilon))

    for phase, buffer in enumerate((send1, send2, send3, send4)):
        part = buffer.at[pl.ds(0, PEERS - 1)]
        pltpu.make_async_remote_copy(
            part, part, xsend.at[phase], xrecv.at[0], device_id={"ent": me}, device_id_type=MESH
        ).wait_send()
    for copy in shifted:
        copy.wait_send()
    for sem, buffer in enumerate((there_src, tg_send, tg_all, og_send, og_all, sg_all)):
        from_reps(buffer, 3 + sem).wait_send()


def write_kernel(table, state, ops, opstate, table_out, state_out, ops_out, opstate_out, sem):
    copies = [
        pltpu.make_async_copy(a, b, sem.at[i])
        for i, (a, b) in enumerate(
            ((table, table_out), (ops, ops_out), (opstate, opstate_out), (state, state_out))
        )
    ]
    for copy in copies:
        copy.start()
    for copy in copies:
        copy.wait()


def shards(
    entity_table,
    entity_state,
    operators,
    operator_state,
    sources,
    destinations,
    relations,
    negatives,
):
    vmem = pl.BlockSpec(memory_space=pltpu.VMEM)
    hbm = pl.BlockSpec(memory_space=pltpu.HBM)
    blocks = pltpu.VMEM((PEERS, 8, 128), BF16)
    whole = CHUNKS * SLOTS
    flat_table = entity_table.T
    results = (
        jax.ShapeDtypeStruct((D, ROWS), F32),
        jax.ShapeDtypeStruct((1, ROWS), F32),
        jax.ShapeDtypeStruct((2, D, D), F32),
        jax.ShapeDtypeStruct((2, D, D), F32),
    )
    fresh = pl.pallas_call(
        step_kernel,
        name="step",
        out_shape=results,
        in_specs=[hbm] * 8,
        out_specs=(vmem,) * 4,
        scratch_shapes=[
            *(pltpu.VMEM(out.shape, F32) for out in results),
            *([pltpu.VMEM((1, EDGES), jnp.int32)] * 3),
            pltpu.VMEM((1, NEG), jnp.int32),
            pltpu.VMEM((256, ROWS), BF16),
            pltpu.VMEM((2, 256, 256), BF16),
            pltpu.VMEM((1, ROWS), jnp.int32),
            pltpu.VMEM((1, EDGES), jnp.int32),
            pltpu.VMEM((1, EDGES), jnp.int32),
            pltpu.VMEM((1, ROWS), jnp.int32),
            pltpu.VMEM((REPS, 1, EDGES), jnp.int32),
            *([blocks] * 8),
            pltpu.VMEM((2, 256, 256), BF16),
            pltpu.VMEM((2, 256, 256), BF16),
            pltpu.VMEM((whole, 256), BF16),
            pltpu.VMEM((whole, 256), BF16),
            pltpu.VMEM((whole, ROWS), BF16),
            pltpu.VMEM((whole, ROWS), BF16),
            pltpu.VMEM((whole, 256), F32),
            pltpu.VMEM((REPS, EDGES, ROWS), BF16),
            *([pltpu.VMEM((REPS, D, 256), BF16)] * 3),
            *([pltpu.VMEM((REPS, HALF, 256), BF16)] * 3),
            pltpu.VMEM((REPS, D, 256), BF16),
            pltpu.SemaphoreType.DMA((8,)),
            pltpu.SemaphoreType.DMA((9,)),
            pltpu.SemaphoreType.DMA((9,)),
            pltpu.SemaphoreType.DMA((4,)),
            pltpu.SemaphoreType.DMA((4 * CHUNKS,)),
        ],
        compiler_params=pltpu.CompilerParams(
            collective_id=0, has_side_effects=True, vmem_limit_bytes=32 << 20
        ),
    )(
        *(
            pltpu.with_memory_space_constraint(array, pltpu.HBM)
            for array in (
                flat_table,
                entity_state.reshape(1, ROWS),
                operators,
                operator_state,
                sources.reshape(1, EDGES),
                destinations.reshape(1, EDGES),
                relations.reshape(1, EDGES),
                negatives,
            )
        )
    )
    table, state, ops, opstate = pl.pallas_call(
        write_kernel,
        name="write",
        out_shape=results,
        in_specs=[vmem] * 4,
        out_specs=(hbm,) * 4,
        scratch_shapes=[pltpu.SemaphoreType.DMA((4,))],
        compiler_params=pltpu.CompilerParams(vmem_limit_bytes=4 << 20),
    )(*fresh)
    return (table.T, state.reshape(ROWS), ops, opstate)


def solution(mesh):
    placed = (
        P("ent", None),
        P("ent"),
        P("ent", None, None),
        P("ent", None, None),
        P(("ent", "rep")),
        P(("ent", "rep")),
        P(("ent", "rep"), None),
        P(("ent", "rep"), None),
    )
    return jax.shard_map(
        shards,
        mesh=mesh,
        in_specs=placed,
        out_specs=(P("ent", None), P("ent"), P("ent", None, None), P("ent", None, None)),
        check_vma=False,
    )
```

```python
import jax
import jax.numpy as jnp
from jax import lax
from jax.experimental import pallas as pl
from jax.experimental.pallas import tpu as pltpu
from jax.sharding import PartitionSpec as P

MESH = pl.DeviceIdType.MESH
F32 = jnp.float32
BF16 = jnp.bfloat16

D = 200
NEG = 1000
ROWS = 1024
EDGES = 256
PEERS = 128
REPS = 4
DEPTH = 16
HALF = 112
CHUNKS = 4
HOPS = (8, -6, 4, -2, 7, -5, 3, -1, -7, 5, -3, 1, 6, -4, 2, 0)
BLOCKS = PEERS // CHUNKS
SLOTS = 4 * BLOCKS
STEPS = DEPTH // CHUNKS
GROUP = 2 * BLOCKS

entity_rate = 0.1
operator_rate = 0.02
epsilon = 1e-06


def dot(a, b):
    return jnp.dot(a, b, preferred_element_type=F32)


def dot_nt(a, b):
    return lax.dot_general(a, b, (((1,), (1,)), ((), ())), preferred_element_type=F32)


def one_hot(index, shape, axis):
    return jnp.where(lax.broadcasted_iota(jnp.int32, shape, axis) == index, 1.0, 0.0).astype(BF16)


def column(row):
    return jnp.transpose(jnp.broadcast_to(row, (128, row.shape[1])))[:, :1]


def split(device):
    return device // (2 * DEPTH), lax.rem(device // 2, DEPTH), lax.rem(device, 2)


def around(device, sign):
    x, z, c = split(device)
    columns = [lax.rem(x + 4 + sign * dx, 4) * (2 * DEPTH) for dx in range(4)]

    def peers(hop, core):
        low = 2 * lax.rem(z + DEPTH + sign * hop, DEPTH) + lax.rem(c + core, 2)
        return [column + low for column in columns]

    return peers


def slot_of(relation, device):
    row = jnp.broadcast_to(relation, (EDGES, EDGES))
    col = jnp.transpose(row)
    sub = lax.broadcasted_iota(jnp.int32, (EDGES, EDGES), 0)
    lane = lax.broadcasted_iota(jnp.int32, (EDGES, EDGES), 1)
    earlier = jnp.sum(
        jnp.where((row == col) & (sub < lane), 1.0, 0.0), axis=0, keepdims=True
    ).astype(jnp.int32)
    x, z, c = split(device)
    owner = relation >> 1
    dx = ((owner >> 5) + 4 - x) & 3
    dz = (((owner >> 1) & 15) + DEPTH - z) & 15
    dc = ((owner & 1) + 2 - c) & 1
    step = sum(jnp.where(dz == hop % DEPTH, i, 0) for i, hop in enumerate(HOPS))
    k = step * 8 + dx * 2 + dc
    return (
        (k // BLOCKS) * SLOTS + (relation & 1) * (2 * BLOCKS) + (k & (BLOCKS - 1)) * 2 + earlier
    )


def block_row(i):
    slot = i & (SLOTS - 1)
    pair = slot & (2 * BLOCKS - 1)
    return (pair >> 1) * 8 + (i // SLOTS) * 4 + (slot // (2 * BLOCKS)) * 2 + (slot & 1)


def step_kernel(
    table_hbm, state_hbm, ops_hbm, opstate_hbm, src_hbm, dst_hbm, rel_hbm, neg_hbm,
    table_out, state_out, ops_out, opstate_out,
    table, state, ops, opstate, src, dst, rel, neg,
    half, ops_half, negs, there_dst, there_rel, there_neg, there_src,
    send1, recv1, send2, recv2, send3, recv3, send4, recv4,
    rows_first, rows_third, moved_all, pulled_all, weights, target_hot, target_rows,
    hits, tg_send, tg_recv, tg_all, og_send, og_recv, og_all, sg_all,
    lsem, ssem, rsem, xsend, xrecv,
):
    me = lax.axis_index("ent")
    y = lax.axis_index("rep")
    nxt = lax.rem(me + 1, PEERS)
    prev = lax.rem(me + PEERS - 1, PEERS)

    onward, backward, onward_prev = around(me, 1), around(me, -1), around(prev, 1)

    loads = [
        pltpu.make_async_copy(a, b, lsem.at[i])
        for i, (a, b) in enumerate(
            (
                (rel_hbm, rel), (src_hbm, src), (dst_hbm, dst),
                (neg_hbm, neg), (table_hbm, table), (ops_hbm, ops),
                (opstate_hbm, opstate), (state_hbm, state),
            )
        )
    ]
    for load in loads:
        load.start()

    barrier = pltpu.get_barrier_semaphore()

    def greet(i, _):
        pl.semaphore_signal(
            barrier, inc=1, device_id={"ent": lax.rem(me + i, PEERS)}, device_id_type=MESH
        )
        return 0

    lax.fori_loop(1, PEERS, greet, 0)
    for i in range(1, REPS):
        pl.semaphore_signal(
            barrier, inc=1, device_id={"rep": lax.rem(y + i, REPS)}, device_id_type=MESH
        )

    def to_reps(source_at, target_at, sem):
        for i in range(1, REPS):
            other = lax.rem(y + i, REPS)
            pltpu.make_async_remote_copy(
                source_at(other), target_at, ssem.at[sem], rsem.at[sem],
                device_id={"rep": other}, device_id_type=MESH,
            ).start()

    def from_reps(ref, sem):
        part = ref.at[pl.ds(0, REPS - 1)]
        return pltpu.make_async_remote_copy(
            part, part, ssem.at[sem], rsem.at[sem], device_id={"rep": y}, device_id_type=MESH
        )

    def send_chunk(phase, g, source, target, peers, late=0, fixed=True):
        def send(core, _):
            for step in range(g * STEPS, (g + 1) * STEPS):
                for dx, peer in enumerate(peers(HOPS[step], core)):
                    k = step * 8 + dx * 2 + core
                    if late:
                        peer = lax.rem(peer + late, PEERS)

                    def away(k=k, peer=peer):
                        pltpu.make_async_remote_copy(
                            source.at[k], target.at[k],
                            xsend.at[phase], xrecv.at[phase * CHUNKS + g],
                            device_id={"ent": peer}, device_id_type=MESH,
                        ).start()

                    def home(k=k):
                        pltpu.make_async_copy(
                            source.at[k], target.at[k], xrecv.at[phase * CHUNKS + g]
                        ).start()

                    if not fixed and HOPS[step] in (0, 1, -1):
                        pl.when(peer != me)(away)
                        pl.when(peer == me)(home)
                    elif fixed and dx == 0 and HOPS[step] == 0:
                        pl.when(core == 1)(away)
                        pl.when(core == 0)(home)
                    else:
                        away()
            return 0

        lax.fori_loop(0, 2, send, 0)

    def wait_chunk(phase, g, target):
        part = target.at[pl.ds(g * BLOCKS, BLOCKS)]
        pltpu.make_async_copy(part, part, xrecv.at[phase * CHUNKS + g]).wait()

    for load in loads[:4]:
        load.wait()
    negs[...] = jnp.full_like(negs, -1)
    negs[:, 0:NEG] = neg[...]
    there_src[y] = src[...]
    slots = slot_of(rel[...], me)
    pack = one_hot(
        block_row(lax.broadcasted_iota(jnp.int32, (8 * BLOCKS, 2 * SLOTS), 1)),
        (8 * BLOCKS, 2 * SLOTS), 0,
    )
    unpack = one_hot(
        block_row(lax.broadcasted_iota(jnp.int32, (2 * SLOTS, 8 * BLOCKS), 0)),
        (2 * SLOTS, 8 * BLOCKS), 1,
    )

    def put(ref, g, value):
        value = value.astype(BF16)
        stacked = jnp.concatenate([value[:, 0:128], value[:, 128:256]], axis=0)
        ref[g * BLOCKS : (g + 1) * BLOCKS] = (
            dot(pack, stacked).reshape(BLOCKS, 8, 128).astype(BF16)
        )

    def get(ref, g):
        flat = ref[g * BLOCKS : (g + 1) * BLOCKS].astype(F32).reshape(8 * BLOCKS, 128)
        both = dot(unpack, flat.astype(BF16))
        return jnp.concatenate([both[0:SLOTS], both[SLOTS : 2 * SLOTS]], axis=1)

    picked = one_hot(src[...], (ROWS, EDGES), 0)
    half[...] = jnp.zeros_like(half)
    ops_half[...] = jnp.zeros_like(ops_half)
    loads[4].wait()
    half[0:D, :] = table[...].astype(BF16)
    source_rows = dot(half[...], picked).astype(BF16)
    for g in range(CHUNKS):
        here = one_hot(slots - g * SLOTS, (SLOTS, EDGES), 0)
        put(send1, g, dot_nt(here, source_rows))

    pl.semaphore_wait(barrier, PEERS - 1 + REPS - 1)

    shifted = [
        pltpu.make_async_remote_copy(
            a, b, ssem.at[i], rsem.at[i], device_id={"ent": nxt}, device_id_type=MESH
        )
        for i, (a, b) in enumerate(((dst, there_dst), (rel, there_rel), (negs, there_neg)))
    ]
    for copy in shifted:
        copy.start()
    to_reps(lambda other: src, there_src.at[y], 3)

    for g in range(CHUNKS):
        send_chunk(0, g, send1, recv1, onward)
    loads[5].wait()
    for r in range(2):
        ops_half[r, 0:D, 0:D] = ops[r].astype(BF16)
    for g in range(CHUNKS):
        wait_chunk(0, g, recv1)
        rows = get(recv1, g).astype(BF16)
        put(
            send2, g,
            jnp.concatenate(
                [dot(rows[GROUP * r : GROUP * (r + 1)], ops_half[r]) for r in range(2)], axis=0
            ),
        )
        send_chunk(1, g, send2, recv2, backward, late=1, fixed=False)
        for r in range(2):
            rows_first[r, GROUP * g : GROUP * (g + 1)] = rows[GROUP * r : GROUP * (r + 1)]

    for copy in shifted:
        copy.wait_recv()
    far_slots = slot_of(there_rel[...], prev)
    for g in range(CHUNKS):
        here = (
            lax.broadcasted_iota(jnp.int32, (SLOTS, EDGES), 0) == far_slots - g * SLOTS
        )
        target = (
            jnp.sum(
                jnp.where(here, (there_dst[...] + 1).astype(F32), 0.0), axis=1, keepdims=True
            ).astype(jnp.int32)
            - 1
        )
        hot = one_hot(target, (SLOTS, ROWS), 1)
        target_hot[g * SLOTS : (g + 1) * SLOTS] = hot
    target_rows[...] = dot_nt(target_hot[...], half[...])
    named = there_neg[...]
    coarse = one_hot(named >> 7, (8, ROWS), 0)
    fine = one_hot(named & 127, (128, ROWS), 0)
    tally = dot_nt(coarse, fine) * (1.0 / NEG)
    tally = jnp.concatenate([tally[j : j + 1] for j in range(8)], axis=1)

    for g in range(CHUNKS):
        span = slice(g * SLOTS, (g + 1) * SLOTS)
        wait_chunk(1, g, recv2)
        moved = get(recv2, g)
        moved_half = moved.astype(BF16)
        scores = dot(moved_half, half[...])
        positive = jnp.sum(
            jnp.where(target_hot[span] > 0, scores, 0.0), axis=1, keepdims=True
        )
        positive_grad = -jax.nn.sigmoid(-positive)
        weight = (tally * jax.nn.sigmoid(scores)).astype(BF16)
        put(send3, g, positive_grad * target_rows[span] + dot_nt(weight, half[...]))
        send_chunk(2, g, send3, recv3, onward_prev, fixed=False)
        weights[span] = weight
        moved_all[span] = moved_half
        pulled_all[span] = (positive_grad * moved).astype(BF16)

    def turned(ref):
        return jnp.transpose(ref.astype(F32)).astype(BF16)

    target_grad = dot(turned(moved_all[...]), weights[...]) + dot(
        turned(pulled_all[...]), target_hot[...]
    )
    for k in range(REPS):
        tg_send[k] = target_grad[0:D, 256 * k : 256 * k + 256].astype(BF16)
    to_reps(lambda other: tg_send.at[other], tg_recv.at[y], 4)

    for g in range(CHUNKS):
        wait_chunk(2, g, recv3)
        rows = get(recv3, g).astype(BF16)
        put(
            send4, g,
            jnp.concatenate(
                [dot_nt(rows[GROUP * r : GROUP * (r + 1)], ops_half[r]) for r in range(2)], axis=0
            ),
        )
        send_chunk(3, g, send4, recv4, backward)
        for r in range(2):
            rows_third[r, GROUP * g : GROUP * (g + 1)] = rows[GROUP * r : GROUP * (r + 1)]

    def summed(sent, received):
        total = sent[y].astype(F32)
        for i in range(1, REPS):
            total = total + received[lax.rem(y + i, REPS)].astype(F32)
        return total.astype(BF16)

    for r in range(2):
        operator_grad = dot(turned(rows_first[r]), rows_third[r])
        og_send[2 * r] = operator_grad[0:HALF].astype(BF16)
        og_send[2 * r + 1] = operator_grad[HALF : 2 * HALF].astype(BF16)
    to_reps(lambda other: og_send.at[other], og_recv.at[y], 6)
    from_reps(tg_recv, 4).wait_recv()
    tg_all[y] = summed(tg_send, tg_recv)
    to_reps(lambda other: tg_all.at[y], tg_all.at[y], 5)
    from_reps(there_src, 3).wait_recv()
    for k in range(REPS):
        hits[k] = one_hot(column(there_src[k]), (EDGES, ROWS), 1)

    slot_col = column(slots)
    takes = [one_hot(slot_col - g * SLOTS, (EDGES, SLOTS), 1) for g in range(CHUNKS)]
    for load in loads[6:]:
        load.wait()

    source_grad = jnp.zeros((EDGES, 256), F32)
    for g in range(CHUNKS):
        wait_chunk(3, g, recv4)
        source_grad = source_grad + dot(takes[g], get(recv4, g).astype(BF16))
    sg_all[y] = jnp.transpose(source_grad)[0:D].astype(BF16)
    to_reps(lambda other: sg_all.at[y], sg_all.at[y], 8)
    from_reps(og_recv, 6).wait_recv()
    og_all[y] = summed(og_send, og_recv)
    to_reps(lambda other: og_all.at[y], og_all.at[y], 7)

    from_reps(tg_all, 5).wait_recv()
    gradient = jnp.concatenate([tg_all[k].astype(F32) for k in range(REPS)], axis=1)
    from_reps(sg_all, 8).wait_recv()
    for k in range(REPS):
        gradient = gradient + dot(sg_all[k], hits[k])
    fresh = state[...] + jnp.sum(gradient * gradient, axis=0, keepdims=True) * (1.0 / D)
    state_out[...] = fresh
    table_out[...] = table[...] - gradient * (entity_rate / (jnp.sqrt(fresh) + epsilon))
    from_reps(og_all, 7).wait_recv()
    for r in range(2):
        for part, (low, high) in enumerate(((0, HALF), (HALF, D))):
            gradient = og_all[2 * r + part][0 : high - low, 0:D].astype(F32)
            fresh = opstate[r, low:high, :] + gradient * gradient
            opstate_out[r, low:high, :] = fresh
            ops_out[r, low:high, :] = ops[r, low:high, :] - (
                operator_rate * gradient / (jnp.sqrt(fresh) + epsilon)
            )

    for phase, buffer in enumerate((send1, send2, send3, send4)):
        part = buffer.at[pl.ds(0, PEERS - 1)]
        pltpu.make_async_remote_copy(
            part, part, xsend.at[phase], xrecv.at[0], device_id={"ent": me}, device_id_type=MESH
        ).wait_send()
    for copy in shifted:
        copy.wait_send()
    for sem, buffer in enumerate((there_src, tg_send, tg_all, og_send, og_all, sg_all)):
        from_reps(buffer, 3 + sem).wait_send()


def write_kernel(table, state, ops, opstate, table_out, state_out, ops_out, opstate_out, sem):
    copies = [
        pltpu.make_async_copy(a, b, sem.at[i])
        for i, (a, b) in enumerate(
            ((table, table_out), (ops, ops_out), (opstate, opstate_out), (state, state_out))
        )
    ]
    for copy in copies:
        copy.start()
    for copy in copies:
        copy.wait()


def shards(
    entity_table,
    entity_state,
    operators,
    operator_state,
    sources,
    destinations,
    relations,
    negatives,
):
    vmem = pl.BlockSpec(memory_space=pltpu.VMEM)
    hbm = pl.BlockSpec(memory_space=pltpu.HBM)
    blocks = pltpu.VMEM((PEERS, 8, 128), BF16)
    whole = CHUNKS * SLOTS
    flat_table = entity_table.T
    results = (
        jax.ShapeDtypeStruct((D, ROWS), F32),
        jax.ShapeDtypeStruct((1, ROWS), F32),
        jax.ShapeDtypeStruct((2, D, D), F32),
        jax.ShapeDtypeStruct((2, D, D), F32),
    )
    fresh = pl.pallas_call(
        step_kernel,
        name="step",
        out_shape=results,
        in_specs=[hbm] * 8,
        out_specs=(vmem,) * 4,
        scratch_shapes=[
            *(pltpu.VMEM(out.shape, F32) for out in results),
            *([pltpu.VMEM((1, EDGES), jnp.int32)] * 3),
            pltpu.VMEM((1, NEG), jnp.int32),
            pltpu.VMEM((256, ROWS), BF16),
            pltpu.VMEM((2, 256, 256), BF16),
            pltpu.VMEM((1, ROWS), jnp.int32),
            pltpu.VMEM((1, EDGES), jnp.int32),
            pltpu.VMEM((1, EDGES), jnp.int32),
            pltpu.VMEM((1, ROWS), jnp.int32),
            pltpu.VMEM((REPS, 1, EDGES), jnp.int32),
            *([blocks] * 8),
            pltpu.VMEM((2, 256, 256), BF16),
            pltpu.VMEM((2, 256, 256), BF16),
            pltpu.VMEM((whole, 256), BF16),
            pltpu.VMEM((whole, 256), BF16),
            pltpu.VMEM((whole, ROWS), BF16),
            pltpu.VMEM((whole, ROWS), BF16),
            pltpu.VMEM((whole, 256), F32),
            pltpu.VMEM((REPS, EDGES, ROWS), BF16),
            *([pltpu.VMEM((REPS, D, 256), BF16)] * 3),
            *([pltpu.VMEM((REPS, HALF, 256), BF16)] * 3),
            pltpu.VMEM((REPS, D, 256), BF16),
            pltpu.SemaphoreType.DMA((8,)),
            pltpu.SemaphoreType.DMA((9,)),
            pltpu.SemaphoreType.DMA((9,)),
            pltpu.SemaphoreType.DMA((4,)),
            pltpu.SemaphoreType.DMA((4 * CHUNKS,)),
        ],
        compiler_params=pltpu.CompilerParams(
            collective_id=0, has_side_effects=True, vmem_limit_bytes=32 << 20
        ),
    )(
        *(
            pltpu.with_memory_space_constraint(array, pltpu.HBM)
            for array in (
                flat_table,
                entity_state.reshape(1, ROWS),
                operators,
                operator_state,
                sources.reshape(1, EDGES),
                destinations.reshape(1, EDGES),
                relations.reshape(1, EDGES),
                negatives,
            )
        )
    )
    table, state, ops, opstate = pl.pallas_call(
        write_kernel,
        name="write",
        out_shape=results,
        in_specs=[vmem] * 4,
        out_specs=(hbm,) * 4,
        scratch_shapes=[pltpu.SemaphoreType.DMA((4,))],
        compiler_params=pltpu.CompilerParams(vmem_limit_bytes=4 << 20),
    )(*fresh)
    return (table.T, state.reshape(ROWS), ops, opstate)


def solution(mesh):
    placed = (
        P("ent", None),
        P("ent"),
        P("ent", None, None),
        P("ent", None, None),
        P(("ent", "rep")),
        P(("ent", "rep")),
        P(("ent", "rep"), None),
        P(("ent", "rep"), None),
    )
    return jax.shard_map(
        shards,
        mesh=mesh,
        in_specs=placed,
        out_specs=(P("ent", None), P("ent"), P("ent", None, None), P("ent", None, None)),
        check_vma=False,
    )
```

```python
import jax
import jax.numpy as jnp
from jax import lax
from jax.experimental import pallas as pl
from jax.experimental.pallas import tpu as pltpu
from jax.sharding import PartitionSpec as P

MESH = pl.DeviceIdType.MESH
F32 = jnp.float32
BF16 = jnp.bfloat16

D = 200
NEG = 1000
ROWS = 1024
EDGES = 256
PEERS = 128
REPS = 4
DEPTH = 16
HALF = 112
CHUNKS = 4
HOPS = (8, -6, 4, -2, 7, -5, 3, -1, -7, 5, -3, 1, 6, -4, 2, 0)
BLOCKS = PEERS // CHUNKS
SLOTS = 4 * BLOCKS
STEPS = DEPTH // CHUNKS
GROUP = 2 * BLOCKS

entity_rate = 0.1
operator_rate = 0.02
epsilon = 1e-06


def dot(a, b):
    return jnp.dot(a, b, preferred_element_type=F32)


def dot_nt(a, b):
    return lax.dot_general(a, b, (((1,), (1,)), ((), ())), preferred_element_type=F32)


def one_hot(index, shape, axis):
    return jnp.where(lax.broadcasted_iota(jnp.int32, shape, axis) == index, 1.0, 0.0).astype(BF16)


def column(row):
    return jnp.transpose(jnp.broadcast_to(row, (128, row.shape[1])))[:, :1]


def split(device):
    return device // (2 * DEPTH), lax.rem(device // 2, DEPTH), lax.rem(device, 2)


def around(device, sign):
    x, z, c = split(device)
    columns = [lax.rem(x + 4 + sign * dx, 4) * (2 * DEPTH) for dx in range(4)]

    def peers(hop, core):
        low = 2 * lax.rem(z + DEPTH + sign * hop, DEPTH) + lax.rem(c + core, 2)
        return [column + low for column in columns]

    return peers


def slot_of(relation, device):
    row = jnp.broadcast_to(relation, (EDGES, EDGES))
    col = jnp.transpose(row)
    sub = lax.broadcasted_iota(jnp.int32, (EDGES, EDGES), 0)
    lane = lax.broadcasted_iota(jnp.int32, (EDGES, EDGES), 1)
    earlier = jnp.sum(
        jnp.where((row == col) & (sub < lane), 1.0, 0.0), axis=0, keepdims=True
    ).astype(jnp.int32)
    x, z, c = split(device)
    owner = relation >> 1
    dx = ((owner >> 5) + 4 - x) & 3
    dz = (((owner >> 1) & 15) + DEPTH - z) & 15
    dc = ((owner & 1) + 2 - c) & 1
    step = sum(jnp.where(dz == hop % DEPTH, i, 0) for i, hop in enumerate(HOPS))
    k = step * 8 + dx * 2 + dc
    return (
        (k // BLOCKS) * SLOTS + (relation & 1) * (2 * BLOCKS) + (k & (BLOCKS - 1)) * 2 + earlier
    )


def block_row(i):
    slot = i & (SLOTS - 1)
    pair = slot & (2 * BLOCKS - 1)
    return (pair >> 1) * 8 + (i // SLOTS) * 4 + (slot // (2 * BLOCKS)) * 2 + (slot & 1)


def step_kernel(
    table_hbm, state_hbm, ops_hbm, opstate_hbm, src_hbm, dst_hbm, rel_hbm, neg_hbm,
    table_out, state_out, ops_out, opstate_out,
    table, state, ops, opstate, src, dst, rel, neg,
    half, ops_half, negs, there_dst, there_rel, there_neg, there_src,
    send1, recv1, send2, recv2, send3, recv3, send4, recv4,
    rows_first, rows_third, moved_all, pulled_all, weights, target_hot, target_rows,
    hits, tg_send, tg_recv, tg_all, og_send, og_recv, og_all, sg_all,
    lsem, ssem, rsem, gsend, grecv, xsend, xrecv,
):
    me = lax.axis_index("ent")
    y = lax.axis_index("rep")
    nxt = lax.rem(me + 1, PEERS)
    prev = lax.rem(me + PEERS - 1, PEERS)

    onward, backward, onward_prev = around(me, 1), around(me, -1), around(prev, 1)

    loads = [
        pltpu.make_async_copy(a, b, lsem.at[i])
        for i, (a, b) in enumerate(
            (
                (rel_hbm, rel), (src_hbm, src), (dst_hbm, dst),
                (neg_hbm, neg), (table_hbm, table), (ops_hbm, ops),
                (opstate_hbm, opstate), (state_hbm, state),
            )
        )
    ]
    for load in loads:
        load.start()

    barrier = pltpu.get_barrier_semaphore()

    def greet(core, _):
        for far in (8, 7, -7, 6, -6, 5, -5, 4, -4, 3, -3, 2, -2, 1, -1, 0):
            for dx, peer in enumerate(onward(far, core)):

                def signal(peer=peer):
                    pl.semaphore_signal(
                        barrier, inc=1, device_id={"ent": peer}, device_id_type=MESH
                    )

                if far or dx:
                    signal()
                else:
                    pl.when(core == 1)(signal)
        return 0

    lax.fori_loop(0, 2, greet, 0)
    for i in range(1, REPS):
        pl.semaphore_signal(
            barrier, inc=1, device_id={"rep": lax.rem(y + i, REPS)}, device_id_type=MESH
        )

    def to_reps(source_at, target_at, sem):
        for i in range(1, REPS):
            other = lax.rem(y + i, REPS)
            pltpu.make_async_remote_copy(
                source_at(other), target_at, ssem.at[sem], rsem.at[sem],
                device_id={"rep": other}, device_id_type=MESH,
            ).start()

    def from_reps(ref, sem):
        part = ref.at[pl.ds(0, REPS - 1)]
        return pltpu.make_async_remote_copy(
            part, part, ssem.at[sem], rsem.at[sem], device_id={"rep": y}, device_id_type=MESH
        )

    class Gather:
        def __init__(self, ref, rows, cut, base):
            left, far, right = (lax.rem(y + i, REPS) for i in (3, 2, 1))
            first, rest = pl.ds(0, cut), pl.ds(cut, rows - cut)

            def copy(part, owner, to, i):
                block = ref.at[owner] if part is None else ref.at[owner, part]
                return pltpu.make_async_remote_copy(
                    block, block, gsend.at[base + i], grecv.at[base + i],
                    device_id={"rep": to}, device_id_type=MESH,
                )

            self.copies = [
                copy(first, y, left, 0),
                copy(rest, y, far, 1),
                copy(None, y, right, 2),
                copy(rest, y, left, 3),
                copy(first, right, left, 4),
            ]

        def start(self):
            for each in self.copies[:4]:
                each.start()

        def relay(self):
            self.copies[0].wait_recv()
            self.copies[4].start()

        def arrived(self, *which):
            for i in which:
                self.copies[i].wait_recv()

        def done(self):
            for each in self.copies:
                each.wait_send()

    def send_chunk(phase, g, source, target, peers, late=0, fixed=True):
        def send(core, _):
            for step in range(g * STEPS, (g + 1) * STEPS):
                for dx, peer in enumerate(peers(HOPS[step], core)):
                    k = step * 8 + dx * 2 + core
                    if late:
                        peer = lax.rem(peer + late, PEERS)

                    def away(k=k, peer=peer):
                        pltpu.make_async_remote_copy(
                            source.at[k], target.at[k],
                            xsend.at[phase], xrecv.at[phase * CHUNKS + g],
                            device_id={"ent": peer}, device_id_type=MESH,
                        ).start()

                    def home(k=k):
                        pltpu.make_async_copy(
                            source.at[k], target.at[k], xrecv.at[phase * CHUNKS + g]
                        ).start()

                    if not fixed and HOPS[step] in (0, 1, -1):
                        pl.when(peer != me)(away)
                        pl.when(peer == me)(home)
                    elif fixed and dx == 0 and HOPS[step] == 0:
                        pl.when(core == 1)(away)
                        pl.when(core == 0)(home)
                    else:
                        away()
            return 0

        lax.fori_loop(0, 2, send, 0)

    def wait_chunk(phase, g, target):
        part = target.at[pl.ds(g * BLOCKS, BLOCKS)]
        pltpu.make_async_copy(part, part, xrecv.at[phase * CHUNKS + g]).wait()

    for load in loads[:4]:
        load.wait()
    negs[...] = jnp.full_like(negs, -1)
    negs[:, 0:NEG] = neg[...]
    there_src[y] = src[...]
    slots = slot_of(rel[...], me)
    pack = one_hot(
        block_row(lax.broadcasted_iota(jnp.int32, (8 * BLOCKS, 2 * SLOTS), 1)),
        (8 * BLOCKS, 2 * SLOTS), 0,
    )
    unpack = one_hot(
        block_row(lax.broadcasted_iota(jnp.int32, (2 * SLOTS, 8 * BLOCKS), 0)),
        (2 * SLOTS, 8 * BLOCKS), 1,
    )

    def put(ref, g, value):
        value = value.astype(BF16)
        stacked = jnp.concatenate([value[:, 0:128], value[:, 128:256]], axis=0)
        ref[g * BLOCKS : (g + 1) * BLOCKS] = (
            dot(pack, stacked).reshape(BLOCKS, 8, 128).astype(BF16)
        )

    def get(ref, g):
        flat = ref[g * BLOCKS : (g + 1) * BLOCKS].astype(F32).reshape(8 * BLOCKS, 128)
        both = dot(unpack, flat.astype(BF16))
        return jnp.concatenate([both[0:SLOTS], both[SLOTS : 2 * SLOTS]], axis=1)

    picked = one_hot(src[...], (ROWS, EDGES), 0)
    half[...] = jnp.zeros_like(half)
    ops_half[...] = jnp.zeros_like(ops_half)
    loads[4].wait()
    half[0:D, :] = table[...].astype(BF16)
    source_rows = dot(half[...], picked).astype(BF16)
    for g in range(CHUNKS):
        here = one_hot(slots - g * SLOTS, (SLOTS, EDGES), 0)
        put(send1, g, dot_nt(here, source_rows))

    pl.semaphore_wait(barrier, PEERS - 1 + REPS - 1)

    shifted = [
        pltpu.make_async_remote_copy(
            a, b, ssem.at[i], rsem.at[i], device_id={"ent": nxt}, device_id_type=MESH
        )
        for i, (a, b) in enumerate(((dst, there_dst), (rel, there_rel), (negs, there_neg)))
    ]
    for copy in shifted:
        copy.start()
    to_reps(lambda other: src, there_src.at[y], 3)

    for g in range(CHUNKS):
        send_chunk(0, g, send1, recv1, onward)
    loads[5].wait()
    for r in range(2):
        ops_half[r, 0:D, 0:D] = ops[r].astype(BF16)
    for g in range(CHUNKS):
        wait_chunk(0, g, recv1)
        rows = get(recv1, g).astype(BF16)
        put(
            send2, g,
            jnp.concatenate(
                [dot(rows[GROUP * r : GROUP * (r + 1)], ops_half[r]) for r in range(2)], axis=0
            ),
        )
        send_chunk(1, g, send2, recv2, backward, late=1, fixed=False)
        for r in range(2):
            rows_first[r, GROUP * g : GROUP * (g + 1)] = rows[GROUP * r : GROUP * (r + 1)]

    for copy in shifted:
        copy.wait_recv()
    far_slots = slot_of(there_rel[...], prev)
    for g in range(CHUNKS):
        here = (
            lax.broadcasted_iota(jnp.int32, (SLOTS, EDGES), 0) == far_slots - g * SLOTS
        )
        target = (
            jnp.sum(
                jnp.where(here, (there_dst[...] + 1).astype(F32), 0.0), axis=1, keepdims=True
            ).astype(jnp.int32)
            - 1
        )
        hot = one_hot(target, (SLOTS, ROWS), 1)
        target_hot[g * SLOTS : (g + 1) * SLOTS] = hot
    target_rows[...] = dot_nt(target_hot[...], half[...])
    named = there_neg[...]
    coarse = one_hot(named >> 7, (8, ROWS), 0)
    fine = one_hot(named & 127, (128, ROWS), 0)
    tally = dot_nt(coarse, fine) * (1.0 / NEG)
    tally = jnp.concatenate([tally[j : j + 1] for j in range(8)], axis=1)

    for g in range(CHUNKS):
        span = slice(g * SLOTS, (g + 1) * SLOTS)
        wait_chunk(1, g, recv2)
        moved = get(recv2, g)
        moved_half = moved.astype(BF16)
        scores = dot(moved_half, half[...])
        positive = jnp.sum(
            jnp.where(target_hot[span] > 0, scores, 0.0), axis=1, keepdims=True
        )
        positive_grad = -jax.nn.sigmoid(-positive)
        weight = (tally * jax.nn.sigmoid(scores)).astype(BF16)
        put(send3, g, positive_grad * target_rows[span] + dot_nt(weight, half[...]))
        send_chunk(2, g, send3, recv3, onward_prev, fixed=False)
        weights[span] = weight
        moved_all[span] = moved_half
        pulled_all[span] = (positive_grad * moved).astype(BF16)

    def turned(ref):
        return jnp.transpose(ref.astype(F32)).astype(BF16)

    target_grad = dot(turned(moved_all[...]), weights[...]) + dot(
        turned(pulled_all[...]), target_hot[...]
    )
    for k in range(REPS):
        tg_send[k] = target_grad[0:D, 256 * k : 256 * k + 256].astype(BF16)
    to_reps(lambda other: tg_send.at[other], tg_recv.at[y], 4)
    turned_rows = [turned(rows_first[r]) for r in range(2)]
    targets = Gather(tg_all, D, 96, 0)
    operators = Gather(og_all, HALF, 64, 5)
    gradients = Gather(sg_all, D, 96, 10)

    def summed(sent, received):
        total = sent[y].astype(F32)
        for i in range(1, REPS):
            total = total + received[lax.rem(y + i, REPS)].astype(F32)
        return total.astype(BF16)

    for g in range(CHUNKS):
        wait_chunk(2, g, recv3)
        rows = get(recv3, g).astype(BF16)
        for r in range(2):
            rows_third[r, GROUP * g : GROUP * (g + 1)] = rows[GROUP * r : GROUP * (r + 1)]
        put(
            send4, g,
            jnp.concatenate(
                [dot_nt(rows[GROUP * r : GROUP * (r + 1)], ops_half[r]) for r in range(2)], axis=0
            ),
        )
        if g == CHUNKS - 1:
            for r in range(2):
                operator_grad = dot(turned_rows[r], rows_third[r])
                og_send[2 * r] = operator_grad[0:HALF].astype(BF16)
                og_send[2 * r + 1] = operator_grad[HALF : 2 * HALF].astype(BF16)
            to_reps(lambda other: og_send.at[other], og_recv.at[y], 5)
        send_chunk(3, g, send4, recv4, backward)
        if g == CHUNKS - 2:
            from_reps(tg_recv, 4).wait_recv()
            tg_all[y] = summed(tg_send, tg_recv)
            targets.start()

    from_reps(there_src, 3).wait_recv()
    for k in range(REPS):
        hits[k] = one_hot(column(there_src[k]), (EDGES, ROWS), 1)
    slot_col = column(slots)
    takes = [one_hot(slot_col - g * SLOTS, (EDGES, SLOTS), 1) for g in range(CHUNKS)]
    for load in loads[6:]:
        load.wait()
    targets.relay()

    source_grad = jnp.zeros((EDGES, 256), F32)
    for g in range(CHUNKS):
        wait_chunk(3, g, recv4)
        source_grad = source_grad + dot(takes[g], get(recv4, g).astype(BF16))
        if g == CHUNKS - 3:
            from_reps(og_recv, 5).wait_recv()
            og_all[y] = summed(og_send, og_recv)
            operators.start()
        if g == CHUNKS - 2:
            operators.relay()
    sg_all[y] = jnp.transpose(source_grad)[0:D].astype(BF16)
    gradients.start()

    targets.arrived(1, 2, 3, 4)
    gradient = jnp.concatenate([tg_all[k].astype(F32) for k in range(REPS)], axis=1)
    gradient = gradient + dot(sg_all[y], hits[y])
    gradients.relay()
    operators.arrived(1, 2, 3, 4)
    for r in range(2):
        for part, (low, high) in enumerate(((0, HALF), (HALF, D))):
            change = og_all[2 * r + part][0 : high - low, 0:D].astype(F32)
            fresh = opstate[r, low:high, :] + change * change
            opstate_out[r, low:high, :] = fresh
            ops_out[r, low:high, :] = ops[r, low:high, :] - (
                operator_rate * change / (jnp.sqrt(fresh) + epsilon)
            )
    for i, which in ((3, (2,)), (1, (3,)), (2, (1, 4))):
        gradients.arrived(*which)
        other = lax.rem(y + i, REPS)
        gradient = gradient + dot(sg_all[other], hits[other])
    fresh = state[...] + jnp.sum(gradient * gradient, axis=0, keepdims=True) * (1.0 / D)
    state_out[...] = fresh
    table_out[...] = table[...] - gradient * (entity_rate / (jnp.sqrt(fresh) + epsilon))

    for phase, buffer in enumerate((send1, send2, send3, send4)):
        part = buffer.at[pl.ds(0, PEERS - 1)]
        pltpu.make_async_remote_copy(
            part, part, xsend.at[phase], xrecv.at[0], device_id={"ent": me}, device_id_type=MESH
        ).wait_send()
    for copy in shifted:
        copy.wait_send()
    for sem, buffer in enumerate((there_src, tg_send, og_send)):
        from_reps(buffer, 3 + sem).wait_send()
    for each in (targets, operators, gradients):
        each.done()


def write_kernel(table, state, ops, opstate, table_out, state_out, ops_out, opstate_out, sem):
    copies = [
        pltpu.make_async_copy(a, b, sem.at[i])
        for i, (a, b) in enumerate(
            ((table, table_out), (ops, ops_out), (opstate, opstate_out), (state, state_out))
        )
    ]
    for copy in copies:
        copy.start()
    for copy in copies:
        copy.wait()


def shards(
    entity_table,
    entity_state,
    operators,
    operator_state,
    sources,
    destinations,
    relations,
    negatives,
):
    vmem = pl.BlockSpec(memory_space=pltpu.VMEM)
    hbm = pl.BlockSpec(memory_space=pltpu.HBM)
    blocks = pltpu.VMEM((PEERS, 8, 128), BF16)
    whole = CHUNKS * SLOTS
    flat_table = entity_table.T
    results = (
        jax.ShapeDtypeStruct((D, ROWS), F32),
        jax.ShapeDtypeStruct((1, ROWS), F32),
        jax.ShapeDtypeStruct((2, D, D), F32),
        jax.ShapeDtypeStruct((2, D, D), F32),
    )
    fresh = pl.pallas_call(
        step_kernel,
        name="step",
        out_shape=results,
        in_specs=[hbm] * 8,
        out_specs=(vmem,) * 4,
        scratch_shapes=[
            *(pltpu.VMEM(out.shape, F32) for out in results),
            *([pltpu.VMEM((1, EDGES), jnp.int32)] * 3),
            pltpu.VMEM((1, NEG), jnp.int32),
            pltpu.VMEM((256, ROWS), BF16),
            pltpu.VMEM((2, 256, 256), BF16),
            pltpu.VMEM((1, ROWS), jnp.int32),
            pltpu.VMEM((1, EDGES), jnp.int32),
            pltpu.VMEM((1, EDGES), jnp.int32),
            pltpu.VMEM((1, ROWS), jnp.int32),
            pltpu.VMEM((REPS, 1, EDGES), jnp.int32),
            *([blocks] * 8),
            pltpu.VMEM((2, 256, 256), BF16),
            pltpu.VMEM((2, 256, 256), BF16),
            pltpu.VMEM((whole, 256), BF16),
            pltpu.VMEM((whole, 256), BF16),
            pltpu.VMEM((whole, ROWS), BF16),
            pltpu.VMEM((whole, ROWS), BF16),
            pltpu.VMEM((whole, 256), F32),
            pltpu.VMEM((REPS, EDGES, ROWS), BF16),
            *([pltpu.VMEM((REPS, D, 256), BF16)] * 3),
            *([pltpu.VMEM((REPS, HALF, 256), BF16)] * 3),
            pltpu.VMEM((REPS, D, 256), BF16),
            pltpu.SemaphoreType.DMA((8,)),
            pltpu.SemaphoreType.DMA((6,)),
            pltpu.SemaphoreType.DMA((6,)),
            pltpu.SemaphoreType.DMA((15,)),
            pltpu.SemaphoreType.DMA((15,)),
            pltpu.SemaphoreType.DMA((4,)),
            pltpu.SemaphoreType.DMA((4 * CHUNKS,)),
        ],
        compiler_params=pltpu.CompilerParams(
            collective_id=0, has_side_effects=True, vmem_limit_bytes=32 << 20
        ),
    )(
        *(
            pltpu.with_memory_space_constraint(array, pltpu.HBM)
            for array in (
                flat_table,
                entity_state.reshape(1, ROWS),
                operators,
                operator_state,
                sources.reshape(1, EDGES),
                destinations.reshape(1, EDGES),
                relations.reshape(1, EDGES),
                negatives,
            )
        )
    )
    table, state, ops, opstate = pl.pallas_call(
        write_kernel,
        name="write",
        out_shape=results,
        in_specs=[vmem] * 4,
        out_specs=(hbm,) * 4,
        scratch_shapes=[pltpu.SemaphoreType.DMA((4,))],
        compiler_params=pltpu.CompilerParams(vmem_limit_bytes=4 << 20),
    )(*fresh)
    return (table.T, state.reshape(ROWS), ops, opstate)


def solution(mesh):
    placed = (
        P("ent", None),
        P("ent"),
        P("ent", None, None),
        P("ent", None, None),
        P(("ent", "rep")),
        P(("ent", "rep")),
        P(("ent", "rep"), None),
        P(("ent", "rep"), None),
    )
    return jax.shard_map(
        shards,
        mesh=mesh,
        in_specs=placed,
        out_specs=(P("ent", None), P("ent"), P("ent", None, None), P("ent", None, None)),
        check_vma=False,
    )
```
